32 devices in a mesh: tile: 8 (over z, y), chan: 4 (over x, core).
Axes of the slice: x: 2, y: 2, z: 4, core: 2. Of those that a mesh axis runs over, the one named last changes fastest.
Arguments:
- feat: bfloat16 [128, 64, 256], P('tile', 'chan'), may hold values from -6 to 6
- lift: float32 [64], replicated, may hold values from -3 to 3
- dilation4_weight: bfloat16 [3, 3, 64, 64], replicated, may hold values from -0.25 to 0.25
- dilation8_weight: bfloat16 [3, 3, 64, 64], replicated, may hold values from -0.25 to 0.25
- entry_fraction: bfloat16 [2048, 128], P('tile'), may hold values from 0.019897461 to 0.19921875
- entry_target_tile: int32 [2048, 1], P('tile'), may hold values from 0 to 7; in each aligned block of 256 rows (0 to 255, 256 to 511, ...) at most 64 rows name the same one
- entry_owner_tile: int32 [2048], P('tile'), may hold values from 0 to 31
- entry_local_net: int32 [2048], P('tile'), may hold values from 0 to 63
- pin_demand_weight: float32 [2048], P('tile'), may hold values from 0.2 to 2
- pin_local_net: int32 [2048], P('tile'), may hold values from 0 to 63
- pin_global_cell: int32 [2048], P('tile'), may hold values from 0 to 511
Outputs:
- cell_grad: float32 [512], P('tile')
The draws below stay inside these ranges and needn't reach their ends.
Inputs may be any that keep to these rules, and one draw needn't show every extreme that they name: `entry_target_tile`: among the entries of one tile index, at most 64 name the same destination, and in some tile index exactly 64 do.
All inputs are finite; a program needn't handle non-finite values.
Results may differ from the reference program's by a relative error of at most 0.0003.
Values may be sent and summed in bfloat16 or wider, within the bound.
A program may use at most 64 MiB of HBM per device.

```python
import math
import jax
import jax.numpy as jnp
import numpy as np
from jax import lax

FEATURE_CHANNELS = 64
ROWS_DEV = 16
W = 256
ENT_DEV = 256
NET_DEV = 64
PIN_DEV = 256
TILE_DEV = 32
CAP = 64
HEIGHT = 128
TILES = 256
ENTRIES = 2048
NETS = 512
PINS = 2048
CELLS = 512
N_TILE = 8


def touch_ends(values, key, smallest, top_value):
    dims = values.shape
    index_at = [jax.random.randint(jax.random.fold_in(key, axis), (), 0, dims[axis]) for axis in range(len(dims))]
    values = values.at[tuple(index_at)].set(smallest)
    longest = dims.index(max(dims))
    index_at[longest] = (index_at[longest] + 1) % dims[longest]
    return values.at[tuple(index_at)].set(top_value)


def levels(key, extent, cuts, least, top_value):
    factor_of = 1.0
    for dim, parts in cuts:
        steps = jax.random.uniform(jax.random.fold_in(jax.random.fold_in(key, 6), dim), (parts,), jnp.float32, least / len(cuts), top_value / len(cuts))
        factor_of = factor_of * jnp.repeat(jnp.exp(steps), extent[dim] // parts).reshape((-1,) + (1,) * (len(extent) - 1 - dim))
    return factor_of


def assign_block(key, own, number, rows, count, top, reach, skew):
    sequence = jax.random.permutation(key, count)
    heavy_load, ordinary = portions_of(count, rows * top, reach, skew, True), portions_of(count, rows * top, reach, skew, False)
    places = jnp.arange(count)

    def named(lengths, rotation):
        used = int((lengths > 0).sum())
        fixed = max(1, used // 4)
        passed = fixed + (places - fixed + rotation * (used - fixed)) % max(1, count - fixed)
        return jnp.zeros((count,), jnp.int32).at[sequence[jnp.where(places < fixed, places, passed)]].set(jnp.asarray(lengths, jnp.int32))

    lengths = jnp.where(number % 4 == 0, named(heavy_load, number // 4), named(ordinary, number - number // 4 - 1))
    mixed = jax.random.permutation(jax.random.fold_in(own, 3), count)
    donor, receiver = mixed[0:count // 2 * 2:2], mixed[1:count // 2 * 2:2]
    slack = jnp.minimum(lengths[donor] - 1, reach - lengths[receiver]) // 2
    slack = jnp.where((donor == sequence[0]) | (receiver == sequence[0]) | (lengths[receiver] == 0), 0, jnp.maximum(slack, 0))
    passed = jax.random.randint(jax.random.fold_in(own, 4), (count // 2,), 0, 1 << 20) % (slack + 1)
    lengths = lengths.at[donor].add(-passed).at[receiver].add(passed)
    items = jnp.searchsorted(jnp.cumsum(lengths), jnp.arange(rows * top), side="right").astype(jnp.int32)
    grid = items.reshape(top, rows).T
    grid = grid[jax.random.permutation(jax.random.fold_in(own, 1), rows)]
    rotation = jax.random.randint(jax.random.fold_in(own, 2), (rows, 1), 0, top)
    return jnp.take_along_axis(grid, (jnp.arange(top)[None, :] + rotation) % top, axis=1)


def portions_of(amount, total, limit, skew, full):
    weights = [(1 << 20) // math.isqrt(standing ** skew) + 1 for standing in range(1, amount + 1)]
    largest = limit if full else min(limit, max(-(-total // amount), total * weights[0] // sum(weights)))
    least = 1 if total - largest >= amount - 1 else 0
    holding, surplus = [largest] + [least] * (amount - 1), total - largest - least * (amount - 1)
    while surplus > 0:
        movable = [i for i in range(1, amount) if holding[i] < largest] or [i for i in range(1, amount) if holding[i] < limit]
        mass, budget = sum([weights[i] for i in movable]), surplus
        for i in movable:
            extra = min(limit - holding[i], max(1, budget * weights[i] // mass), surplus)
            holding[i] = holding[i] + extra
            surplus = surplus - extra
    return np.array(holding)


def scatter_about(own_key, extent, scale, bound, pieces=(), held_as=jnp.bfloat16):
    array = scale * jax.random.normal(own_key, extent, jnp.float32)
    if pieces:
        array = array * levels(own_key, extent, pieces, -0.22, 0.18)
    return jnp.clip(array, -bound, bound).astype(held_as)


def setup_inputs(seed: int = 0) -> dict:
    seeds = jax.random.split(jax.random.key(seed), 12)
    feat = scatter_about(seeds[0], (HEIGHT, FEATURE_CHANNELS, W), 1.0, 6.0, ((0, 8), (1, 4)))
    lift = scatter_about(seeds[1], (FEATURE_CHANNELS,), 0.5, 3.0, (), jnp.float32)
    dilation4_weight = scatter_about(seeds[2], (3, 3, FEATURE_CHANNELS, FEATURE_CHANNELS), (9 * FEATURE_CHANNELS) ** -0.5, 0.25)
    dilation8_weight = scatter_about(seeds[3], (3, 3, FEATURE_CHANNELS, FEATURE_CHANNELS), (9 * FEATURE_CHANNELS) ** -0.5, 0.25)
    entry_fraction = jnp.clip(jnp.exp(math.log(0.19921875) - 2.3038113 * jax.random.uniform(seeds[4], (ENTRIES, 128), jnp.float32) ** levels(seeds[4], (ENTRIES, 128), ((0, 8),), -0.2, 0.2)), 0.019897461, 0.19921875).astype(jnp.bfloat16)
    entry_target_tile_keys = jax.random.split(jax.random.fold_in(seeds[5], 1), ENTRIES // ENT_DEV)
    entry_target_tile_turns = jax.random.permutation(jax.random.fold_in(seeds[5], 3), ENTRIES // ENT_DEV)
    entry_target_tile = jax.vmap(lambda own, number: assign_block(jax.random.fold_in(seeds[5], 2), own, number, ENT_DEV, N_TILE, 1, CAP, 2))(entry_target_tile_keys, entry_target_tile_turns).reshape((ENTRIES, 1))
    entry_owner_tile = touch_ends(jax.random.randint(seeds[6], (ENTRIES,), 0, TILE_DEV), jax.random.fold_in(seeds[6], 1), 0, TILE_DEV - 1).astype(jnp.int32)
    entry_local_net = touch_ends(jax.random.randint(seeds[7], (ENTRIES,), 0, NET_DEV), jax.random.fold_in(seeds[7], 1), 0, NET_DEV - 1).astype(jnp.int32)
    pin_demand_weight = jnp.clip(jnp.exp(math.log(2.0) - 2.3025851 * jax.random.uniform(seeds[8], (PINS,), jnp.float32) ** levels(seeds[8], (PINS,), ((0, 8),), -0.2, 0.2)), 0.2, 2.0)
    pin_local_net = touch_ends(jax.random.randint(seeds[9], (PINS,), 0, NET_DEV), jax.random.fold_in(seeds[9], 1), 0, NET_DEV - 1).astype(jnp.int32)
    pin_global_cell = touch_ends(jax.random.randint(seeds[10], (PINS,), 0, CELLS), jax.random.fold_in(seeds[10], 1), 0, CELLS - 1).astype(jnp.int32)
    return dict(feat=feat, lift=lift, dilation4_weight=dilation4_weight, dilation8_weight=dilation8_weight, entry_fraction=entry_fraction, entry_target_tile=entry_target_tile, entry_owner_tile=entry_owner_tile, entry_local_net=entry_local_net, pin_demand_weight=pin_demand_weight, pin_local_net=pin_local_net, pin_global_cell=pin_global_cell)


def dilated_result(source, kernel_in, dilation):
    row_total, col_count = source.shape[0], source.shape[1]
    chan_out = kernel_in.shape[3]
    padded = jnp.pad(source, ((dilation, dilation), (dilation, dilation), (0, 0)))
    kernel = kernel_in.astype(jnp.float32)

    def one_block(block_id):
        offset = (block_id * ROWS_DEV).astype(jnp.int32)
        window = lax.dynamic_slice_in_dim(padded, offset, ROWS_DEV + 2 * dilation, 0).astype(jnp.float32)
        running = jnp.zeros((ROWS_DEV, col_count, chan_out), jnp.float32)
        for row_tap in range(3):
            for col_tap in range(3):
                part_in = window[row_tap * dilation:row_tap * dilation + ROWS_DEV, col_tap * dilation:col_tap * dilation + col_count]
                running = running + jnp.einsum("rwc,co->rwo", part_in, kernel[row_tap, col_tap])
        return running

    result = lax.map(one_block, jnp.arange(row_total // ROWS_DEV, dtype=jnp.int32))
    return result.reshape(row_total, col_count, chan_out)


def flipped_kernel(kernel):
    return jnp.transpose(kernel[::-1, ::-1], (0, 1, 3, 2))


def reference(feat, lift, dilation4_weight, dilation8_weight, entry_fraction, entry_target_tile, entry_owner_tile, entry_local_net, pin_demand_weight, pin_local_net, pin_global_cell):
    feat_rows = jnp.transpose(feat, (0, 2, 1))
    pin_owner = (jnp.arange(PINS) // PIN_DEV).astype(jnp.int32)
    net_of_pin = pin_local_net + pin_owner * NET_DEV
    strength = jax.ops.segment_sum(pin_demand_weight, net_of_pin, num_segments=NETS)
    entry_owner = (jnp.arange(ENTRIES) // ENT_DEV).astype(jnp.int32)
    net_of_entry = entry_local_net + entry_owner * NET_DEV
    tile_of_entry = entry_target_tile[:, 0] * TILE_DEV + entry_owner_tile
    frac = entry_fraction.astype(jnp.float32)
    payload = strength[net_of_entry][:, None] * frac
    tiles = jax.ops.segment_sum(payload, tile_of_entry, num_segments=TILES)
    demand = tiles.reshape(N_TILE, ROWS_DEV // 8, W // 16, 8, 16).transpose(0, 1, 3, 2, 4).reshape(HEIGHT, W)
    input_features = (feat_rows.astype(jnp.float32) + demand[:, :, None] * lift[None, None, :]).astype(jnp.bfloat16)
    first_preactivation = dilated_result(input_features, dilation4_weight, 4)
    hidden_features = jax.nn.silu(first_preactivation).astype(jnp.bfloat16)
    second_output = dilated_result(hidden_features, dilation8_weight, 8)
    second_gradient = jax.nn.sigmoid(second_output).astype(jnp.bfloat16)
    hidden_gradient = dilated_result(second_gradient, flipped_kernel(dilation8_weight), 8)
    sigmoid_pre = jax.nn.sigmoid(first_preactivation)
    preactivation_gradient = (hidden_gradient * sigmoid_pre * (1.0 + first_preactivation * (1.0 - sigmoid_pre))).astype(jnp.bfloat16)
    inputs_gradient = dilated_result(preactivation_gradient, flipped_kernel(dilation4_weight), 4)
    grad_demand = jnp.sum(inputs_gradient * lift[None, None, :], axis=2)
    grad_tiles = grad_demand.reshape(N_TILE, ROWS_DEV // 8, 8, W // 16, 16).transpose(0, 1, 3, 2, 4).reshape(TILES, 128)
    entry_grad = jnp.sum(grad_tiles[tile_of_entry] * frac, axis=1)
    grad_net = jax.ops.segment_sum(entry_grad, net_of_entry, num_segments=NETS)
    return jax.ops.segment_sum(grad_net[net_of_pin], pin_global_cell, num_segments=CELLS)
```

```python
import functools

import jax
import jax.numpy as jnp
from jax import lax
from jax.experimental import pallas as pl
from jax.experimental.pallas import tpu as pltpu
from jax.sharding import PartitionSpec as P

MESH = pl.DeviceIdType.MESH
CELL_DEV = 64
TILE_ROWS = 8
TILE_COLS = 16
LANES = 128
HALO = 24
GROUP = 4
F32 = jnp.float32
BF16 = jnp.bfloat16


def split(x, terms):
    parts = []
    for _ in range(terms):
        part = x.astype(BF16)
        parts.append(part)
        x = x - part.astype(F32)
    return parts


def kernel(
    tiles, chans,
    feat, lift, w4, w8, frac, pack,
    out,
    win, gath, inp, pre, hid, sec, gpre, wm1, wm2, wm3, wm4,
    fmask, dbuf, dsend, drecv, demand, gown, gall, csend, crecv,
    fsend_sem, frecv_sem, own_sem, dsend_sem, drecv_sem, gsend_sem, grecv_sem, gown_sem,
    csend_sem, crecv_sem,
):
    ti = lax.axis_index("tile")
    ci = lax.axis_index("chan")
    rows, chan_own, cols = feat.shape
    chan = chan_own * chans
    own_cols = cols // chans
    margin = (LANES - own_cols) // 2
    reach = -(-HALO // rows)
    in_rows = rows + 2 * HALO
    others = tiles * chans - 1

    barrier = pltpu.get_barrier_semaphore()

    def peer(step):
        number = lax.rem(ti * chans + ci + step, tiles * chans)
        return lax.div(number, chans), lax.rem(number, chans)

    def greet(step, carry):
        pl.semaphore_signal(barrier, inc=1, device_id=peer(step), device_id_type=MESH)
        return carry

    lax.fori_loop(1, others + 1, greet, 0)

    flat = feat[...].astype(F32).reshape(rows * chan_own, cols)
    lane = lax.broadcasted_iota(jnp.int32, (1, LANES), 1)
    for k in range(chans):
        first = k * own_cols - margin
        turned = pltpu.roll(flat, (-first) % cols, 1)[:, :LANES]
        inside = (lane + first >= 0) & (lane + first < cols)
        win[k] = jnp.where(inside, turned, 0.0).astype(BF16).reshape(rows, chan_own, LANES)

    pl.semaphore_wait(barrier, others)

    def spans(delta):
        start = HALO - rows * delta
        low = max(0, -start)
        high = min(rows, in_rows - start)
        return low, high - low, start + low

    def feat_copy(delta, k):
        low, count, at = spans(delta)
        to = lax.rem(ci + k, chans)
        src = win.at[to, pl.ds(low, count)]
        dst = gath.at[pl.ds(at, count), pl.ds(pl.multiple_of(ci * chan_own, chan_own), chan_own)]
        if delta == 0 and k == 0:
            return pltpu.make_async_copy(src, dst, own_sem)
        return pltpu.make_async_remote_copy(
            src_ref=src, dst_ref=dst,
            send_sem=fsend_sem.at[delta + reach, k], recv_sem=frecv_sem.at[delta + reach, k],
            device_id=(ti + delta, to), device_id_type=MESH,
        )

    def feat_arrival(delta, k):
        low, count, at = spans(delta)
        come = lax.rem(ci + chans - k, chans)
        dst = gath.at[pl.ds(at, count), pl.ds(pl.multiple_of(come * chan_own, chan_own), chan_own)]
        return pltpu.make_async_remote_copy(
            src_ref=dst, dst_ref=dst,
            send_sem=fsend_sem.at[delta + reach, k], recv_sem=frecv_sem.at[delta + reach, k],
            device_id=(ti, lax.rem(ci + 1, chans)), device_id_type=MESH,
        )

    order = [(d, k) for d in sorted(range(-reach, reach + 1), key=lambda d: -abs(d)) for k in range(chans)]
    for delta, k in order:
        if delta == 0:
            feat_copy(delta, k).start()
        else:
            @pl.when((ti + delta >= 0) & (ti + delta < tiles))
            def _(delta=delta, k=k):
                feat_copy(delta, k).start()

    table = pack[...]
    columns = jnp.transpose(table)
    entries = table.shape[1]
    net_e_col, wpin_col, net_p_col = columns[:, 2:3], columns[:, 3:4], columns[:, 4:5]
    strength = jnp.sum(
        jnp.where(net_p_col == table[2:3, :], wpin_col, 0.0), axis=0, keepdims=True
    )
    src_j = lax.broadcasted_iota(jnp.int32, (LANES, TILE_ROWS * LANES), 0)
    dst_j = lax.broadcasted_iota(jnp.int32, (LANES, TILE_ROWS * LANES), 1)
    pick = src_j == (dst_j // LANES) * TILE_COLS + dst_j % TILE_COLS
    spread = jnp.dot(
        frac[...], jnp.where(pick, 1.0, 0.0).astype(BF16), preferred_element_type=F32
    )
    wide = lax.broadcasted_iota(jnp.int32, (1, TILE_ROWS * LANES), 1) % LANES
    block = (wide + ci * own_cols - margin + TILE_COLS * LANES) // TILE_COLS - LANES
    fmask[...] = jnp.where(columns[:, 1:2] == block.astype(F32), spread, 0.0).astype(BF16)
    pad_blocks = HALO // TILE_ROWS
    blocks = dbuf.shape[0] // TILE_ROWS
    block_row = lax.broadcasted_iota(jnp.int32, (blocks, entries), 0).astype(F32)
    placed = jnp.where(block_row == table[0:1, :] + float(pad_blocks), strength, 0.0)
    left = jnp.concatenate(split(placed, 2), axis=0)
    partial = jnp.dot(left, fmask[...], preferred_element_type=F32)
    partial = partial[:blocks] + partial[blocks:]
    for i in range(TILE_ROWS):
        dbuf[pl.ds(i, blocks, stride=TILE_ROWS), :] = partial[:, i * LANES : (i + 1) * LANES]
    dsend[...] = dbuf[...].astype(BF16)

    def demand_copy(step):
        to = lax.rem(ti + step, tiles)
        return pltpu.make_async_remote_copy(
            src_ref=dsend.at[pl.ds(pl.multiple_of(to * rows, rows), in_rows)],
            dst_ref=drecv.at[step],
            send_sem=dsend_sem.at[step], recv_sem=drecv_sem.at[step],
            device_id=(to, ci), device_id_type=MESH,
        )

    def each(lo, hi, fn):
        def body(step, carry):
            fn(step)
            return carry
        lax.fori_loop(lo, hi, body, 0)

    each(1, tiles, lambda s: demand_copy(s).start())

    lift_row = lift[...]
    lift_col = jnp.transpose(jnp.broadcast_to(lift_row, (LANES, chan)))
    for u in range(3):
        for v in range(3):
            at_v, at_u = slice(v * chan, (v + 1) * chan), slice(u * chan, (u + 1) * chan)
            wm1[at_v, at_u] = jnp.transpose(w4[u, v].astype(F32)).astype(BF16)
            wm2[at_v, at_u] = jnp.transpose(w8[u, v].astype(F32)).astype(BF16)
            wm3[at_v, at_u] = w8[2 - u, 2 - v]
    taps = []
    for v in range(3):
        taps.append(
            jnp.concatenate(
                [
                    jnp.sum(
                        w4[2 - u, 2 - v].astype(F32) * lift_col[:, :chan], axis=0, keepdims=True
                    )
                    for u in range(3)
                ],
                axis=1,
            )
        )
    tap_rows = jnp.concatenate(taps + [jnp.zeros((5, 3 * chan), F32)], axis=0)
    hi, mid, low_part = [p.astype(F32) for p in split(tap_rows, 3)]
    wm4[...] = jnp.concatenate(
        [hi, mid, low_part, jnp.zeros((8, 3 * chan), F32)], axis=0
    ).astype(BF16)

    each(1, tiles, lambda s: demand_copy(s).wait())
    total = dsend[pl.ds(pl.multiple_of(ti * rows, rows), in_rows), :].astype(F32)
    total = lax.fori_loop(1, tiles, lambda s, t: t + drecv[s].astype(F32), total)
    demand[...] = total

    for delta, k in order:
        if delta == 0:
            if k == 0:
                feat_copy(delta, k).wait()
            else:
                feat_copy(delta, k).wait_send()
                feat_arrival(delta, k).wait_recv()
        else:
            @pl.when((ti + delta >= 0) & (ti + delta < tiles))
            def _(delta=delta, k=k):
                feat_copy(delta, k).wait_send()

            @pl.when((ti - delta >= 0) & (ti - delta < tiles))
            def _(delta=delta, k=k):
                feat_arrival(delta, k).wait_recv()

    height = rows * tiles
    top = ti * rows

    def in_map(row):
        return (row >= 0) & (row < height)

    def fill(g, carry):
        at = g * GROUP
        ok = in_map(top - HALO + at)

        @pl.when(ok)
        def _():
            for j in range(GROUP):
                add = lift_col * demand[pl.ds(at + j, 1), :]
                inp[at + j] = (gath[at + j].astype(F32) + add).astype(BF16)

        @pl.when(jnp.logical_not(ok))
        def _():
            for j in range(GROUP):
                inp[at + j] = jnp.zeros((chan, LANES), BF16)

        return carry

    lax.fori_loop(0, in_rows // GROUP, fill, 0)

    col = lane + ci * own_cols - margin
    col_ok = ((col >= 0) & (col < cols)).astype(F32)

    def gathered(ref, at, dilation):
        return jnp.concatenate(
            [
                jnp.concatenate([ref[at + j + u * dilation] for u in range(3)], axis=0)
                for j in range(GROUP)
            ],
            axis=1,
        )

    def conv(ref, at, weights, dilation):
        result = jnp.dot(weights[...], gathered(ref, at, dilation), preferred_element_type=F32)
        parts = []
        for j in range(GROUP):
            one = result[:, j * LANES : (j + 1) * LANES]
            parts.append(
                one[chan : 2 * chan]
                + pltpu.roll(one[:chan], dilation, 1)
                + pltpu.roll(one[2 * chan :], LANES - dilation, 1)
            )
        return parts

    def keep_of(row):
        return col_ok * in_map(row).astype(F32)

    def first(g, carry):
        at = g * GROUP
        keep = keep_of(top - 20 + at)
        for j, value in enumerate(conv(inp, at, wm1, 4)):
            pre[at + j] = value
            hid[at + j] = (value * jax.nn.sigmoid(value) * keep).astype(BF16)
        return carry

    def second(g, carry):
        at = g * GROUP
        keep = keep_of(top - 12 + at)
        for j, value in enumerate(conv(hid, at, wm2, 8)):
            sec[at + j] = (jax.nn.sigmoid(value) * keep).astype(BF16)
        return carry

    def third(g, carry):
        at = g * GROUP
        keep = keep_of(top - 4 + at)
        for j, value in enumerate(conv(sec, at, wm3, 8)):
            p = pre[at + j + 16]
            s = jax.nn.sigmoid(p)
            gpre[at + j] = (value * s * (1.0 + p * (1.0 - s)) * keep).astype(BF16)
        return carry

    lax.fori_loop(0, (rows + 40) // GROUP, first, 0)
    lax.fori_loop(0, (rows + 24) // GROUP, second, 0)
    lax.fori_loop(0, (rows + 8) // GROUP, third, 0)

    owned = ((lane >= margin) & (lane < margin + own_cols)).astype(F32)
    for g in range(rows // GROUP):
        at = g * GROUP
        result = jnp.dot(wm4[...], gathered(gpre, at, 4), preferred_element_type=F32)
        result = result[0:8] + result[8:16] + result[16:24]
        for j in range(GROUP):
            one = result[:, j * LANES : (j + 1) * LANES]
            line = (
                one[1:2]
                + pltpu.roll(one, 4, 1)[0:1]
                + pltpu.roll(one, LANES - 4, 1)[2:3]
            )
            gown[at + j : at + j + 1, :] = line * owned

    def grad_copy(step):
        to = lax.rem(ti + step, tiles)
        return pltpu.make_async_remote_copy(
            src_ref=gown, dst_ref=gall.at[pl.ds(pl.multiple_of(ti * rows, rows), rows)],
            send_sem=gsend_sem.at[step], recv_sem=grecv_sem.at[step],
            device_id=(to, ci), device_id_type=MESH,
        )

    def grad_arrival(step):
        come = lax.rem(ti + tiles - step, tiles)
        dst = gall.at[pl.ds(pl.multiple_of(come * rows, rows), rows)]
        return pltpu.make_async_remote_copy(
            src_ref=gown, dst_ref=dst,
            send_sem=gsend_sem.at[step], recv_sem=grecv_sem.at[step],
            device_id=(lax.rem(ti + step, tiles), ci), device_id_type=MESH,
        )

    each(1, tiles, lambda s: grad_copy(s).start())
    mine = pltpu.make_async_copy(
        gown, gall.at[pl.ds(pl.multiple_of(ti * rows, rows), rows)], gown_sem
    )
    mine.start()
    map_blocks = height // TILE_ROWS
    block_lane = lax.broadcasted_iota(jnp.int32, (entries, map_blocks), 1).astype(F32)
    block_hot = jnp.where(columns[:, 0:1] == block_lane, 1.0, 0.0).astype(BF16)
    mine.wait()
    each(1, tiles, lambda s: grad_copy(s).wait_send())
    each(1, tiles, lambda s: grad_arrival(s).wait_recv())

    entry_sum = jnp.zeros((entries, LANES), F32)
    for i in range(TILE_ROWS):
        grads = gall[pl.ds(i, map_blocks, stride=TILE_ROWS), :]
        high, low_ = split(grads, 2)
        rows_of = jnp.dot(block_hot, high, preferred_element_type=F32)
        rows_of = rows_of + jnp.dot(block_hot, low_, preferred_element_type=F32)
        entry_sum = entry_sum + rows_of * fmask[:, i * LANES : (i + 1) * LANES].astype(F32)
    entry_grad = jnp.sum(entry_sum, axis=1, keepdims=True)
    pin_grad = jnp.sum(
        jnp.where(net_e_col == table[4:5, :], entry_grad, 0.0), axis=0, keepdims=True
    )
    dest_rows = max(8, tiles)
    dest_row = lax.broadcasted_iota(jnp.int32, (dest_rows, entries), 0).astype(F32)
    cell_row = lax.broadcasted_iota(jnp.int32, (LANES, entries), 0).astype(F32)
    by_dest = jnp.where(dest_row == table[5:6, :], pin_grad, 0.0)
    by_cell = jnp.where(cell_row == table[6:7, :], 1.0, 0.0).astype(BF16)
    pieces = jnp.concatenate([p.astype(F32) for p in split(by_dest, 3)], axis=0).astype(BF16)
    cells = lax.dot_general(
        pieces, by_cell, (((1,), (1,)), ((), ())), preferred_element_type=F32
    )
    cells = cells[:dest_rows] + cells[dest_rows : 2 * dest_rows] + cells[2 * dest_rows :]
    for t in range(tiles):
        csend[t] = cells[t : t + 1, :]

    def cell_copy(step):
        to = peer(step)
        return pltpu.make_async_remote_copy(
            src_ref=csend.at[to[0]], dst_ref=crecv.at[step],
            send_sem=csend_sem.at[step], recv_sem=crecv_sem.at[step],
            device_id=to, device_id_type=MESH,
        )

    each(1, others + 1, lambda s: cell_copy(s).start())
    each(1, others + 1, lambda s: cell_copy(s).wait())
    out[...] = lax.fori_loop(1, others + 1, lambda s, t: t + crecv[s], csend[ti])


def solution(mesh):
    tiles, chans = mesh.shape["tile"], mesh.shape["chan"]

    def local(
        feat, lift, w4, w8, frac, target, owner, net_e, weight, net_p, cell,
    ):
        rows, chan_own, cols = feat.shape
        chan = chan_own * chans
        entries = frac.shape[0]
        per_row = cols // TILE_COLS
        per_strip = rows // TILE_ROWS
        pack = jnp.stack(
            [
                (target[:, 0] * per_strip + owner // per_row).astype(F32),
                (owner % per_row).astype(F32),
                net_e.astype(F32),
                weight,
                net_p.astype(F32),
                (cell // CELL_DEV).astype(F32),
                (cell % CELL_DEV).astype(F32),
                jnp.zeros_like(weight),
            ]
        )
        in_rows = rows + 2 * HALO
        reach = -(-HALO // rows)
        height = rows * tiles
        blocks = -(-(height + 2 * HALO) // (8 * TILE_ROWS)) * 8
        vm = pltpu.VMEM
        dma = pltpu.SemaphoreType.DMA
        result = pl.pallas_call(
            functools.partial(kernel, tiles, chans),
            out_shape=jax.ShapeDtypeStruct((1, LANES), F32),
            in_specs=[pl.BlockSpec(memory_space=pltpu.VMEM)] * 6,
            out_specs=pl.BlockSpec(memory_space=pltpu.VMEM),
            scratch_shapes=[
                vm((chans, rows, chan_own, LANES), BF16),
                vm((in_rows, chan, LANES), BF16),
                vm((in_rows, chan, LANES), BF16),
                vm((rows + 40, chan, LANES), F32),
                vm((rows + 40, chan, LANES), BF16),
                vm((rows + 24, chan, LANES), BF16),
                vm((rows + 8, chan, LANES), BF16),
                vm((3 * chan, 3 * chan), BF16),
                vm((3 * chan, 3 * chan), BF16),
                vm((3 * chan, 3 * chan), BF16),
                vm((32, 3 * chan), BF16),
                vm((entries, TILE_ROWS * LANES), BF16),
                vm((blocks * TILE_ROWS, LANES), F32),
                vm((blocks * TILE_ROWS, LANES), BF16),
                vm((tiles, in_rows, LANES), BF16),
                vm((in_rows, LANES), F32),
                vm((rows, LANES), F32),
                vm((height, LANES), F32),
                vm((tiles, 1, LANES), F32),
                vm((tiles * chans, 1, LANES), F32),
                dma((2 * reach + 1, chans)),
                dma((2 * reach + 1, chans)),
                dma(()),
                dma((tiles,)),
                dma((tiles,)),
                dma((tiles,)),
                dma((tiles,)),
                dma(()),
                dma((tiles * chans,)),
                dma((tiles * chans,)),
            ],
            compiler_params=pltpu.CompilerParams(collective_id=0, has_side_effects=True),
        )(feat, lift.reshape(1, chan), w4, w8, frac, pack)
        return result[0, :CELL_DEV]

    in_specs = (
        P("tile", "chan", None), P(), P(), P(),
        P("tile", None), P("tile", None),
        P("tile"), P("tile"), P("tile"), P("tile"), P("tile"),
    )
    return jax.shard_map(
        local, mesh=mesh, in_specs=in_specs, out_specs=P("tile"), check_vma=False
    )
```

```python
import functools

import jax
import jax.numpy as jnp
from jax import lax
from jax.experimental import pallas as pl
from jax.experimental.pallas import tpu as pltpu
from jax.sharding import PartitionSpec as P

MESH = pl.DeviceIdType.MESH
CELL_DEV = 64
TILE_ROWS = 8
TILE_COLS = 16
LANES = 128
HALO = 24
GROUP = 4
F32 = jnp.float32
BF16 = jnp.bfloat16


def split(x, terms):
    parts = []
    for _ in range(terms):
        part = x.astype(BF16)
        parts.append(part)
        x = x - part.astype(F32)
    return parts


def kernel(
    tiles, chans,
    feat_in, lift_in, w4_in, w8_in, frac_in, target_in, owner_in, net_e_in, weight_in, net_p_in,
    cell_in,
    out,
    feat, lift, w4, w8, frac, target, owner, net_e, weight, net_p, cell, load_sem,
    win, gath, inp, pre, hid, sec, gpre, wm1, wm2, wm3, wm4,
    fmask, dbuf, dsend, drecv, demand, gown, gall, csend, crecv,
    fsend_sem, frecv_sem, own_sem, dsend_sem, drecv_sem, gsend_sem, grecv_sem, gown_sem,
    csend_sem, crecv_sem,
):
    ti = lax.axis_index("tile")
    ci = lax.axis_index("chan")
    rows, chan_own, cols = feat.shape
    chan = chan_own * chans
    own_cols = cols // chans
    margin = (LANES - own_cols) // 2
    reach = -(-HALO // rows)
    in_rows = rows + 2 * HALO
    others = tiles * chans - 1

    loads = [
        pltpu.make_async_copy(src, dst, load_sem.at[n])
        for n, (src, dst) in enumerate(
            [
                (feat_in, feat), (target_in, target), (owner_in, owner), (net_e_in, net_e),
                (weight_in, weight), (net_p_in, net_p), (frac_in, frac), (lift_in, lift),
                (cell_in, cell), (w4_in, w4), (w8_in, w8),
            ]
        )
    ]
    for load in loads:
        load.start()

    barrier = pltpu.get_barrier_semaphore()

    def peer(step):
        number = lax.rem(ti * chans + ci + step, tiles * chans)
        return lax.div(number, chans), lax.rem(number, chans)

    def greet(step, carry):
        pl.semaphore_signal(barrier, inc=1, device_id=peer(step), device_id_type=MESH)
        return carry

    lax.fori_loop(1, others + 1, greet, 0)

    loads[0].wait()

    flat = feat[...].astype(F32).reshape(rows * chan_own, cols)
    lane = lax.broadcasted_iota(jnp.int32, (1, LANES), 1)
    for k in range(chans):
        first = k * own_cols - margin
        turned = pltpu.roll(flat, (-first) % cols, 1)[:, :LANES]
        inside = (lane + first >= 0) & (lane + first < cols)
        win[k] = jnp.where(inside, turned, 0.0).astype(BF16).reshape(rows, chan_own, LANES)

    pl.semaphore_wait(barrier, others)

    def spans(delta):
        start = HALO - rows * delta
        low = max(0, -start)
        high = min(rows, in_rows - start)
        return low, high - low, start + low

    def feat_copy(delta, k):
        low, count, at = spans(delta)
        to = lax.rem(ci + k, chans)
        src = win.at[to, pl.ds(low, count)]
        dst = gath.at[pl.ds(at, count), pl.ds(pl.multiple_of(ci * chan_own, chan_own), chan_own)]
        if delta == 0 and k == 0:
            return pltpu.make_async_copy(src, dst, own_sem)
        return pltpu.make_async_remote_copy(
            src_ref=src, dst_ref=dst,
            send_sem=fsend_sem.at[delta + reach, k], recv_sem=frecv_sem.at[delta + reach, k],
            device_id=(ti + delta, to), device_id_type=MESH,
        )

    def feat_arrival(delta, k):
        low, count, at = spans(delta)
        come = lax.rem(ci + chans - k, chans)
        dst = gath.at[pl.ds(at, count), pl.ds(pl.multiple_of(come * chan_own, chan_own), chan_own)]
        return pltpu.make_async_remote_copy(
            src_ref=dst, dst_ref=dst,
            send_sem=fsend_sem.at[delta + reach, k], recv_sem=frecv_sem.at[delta + reach, k],
            device_id=(ti, lax.rem(ci + 1, chans)), device_id_type=MESH,
        )

    order = [(d, k) for d in sorted(range(-reach, reach + 1), key=lambda d: -abs(d)) for k in range(chans)]
    for delta, k in order:
        if delta == 0:
            feat_copy(delta, k).start()
        else:
            @pl.when((ti + delta >= 0) & (ti + delta < tiles))
            def _(delta=delta, k=k):
                feat_copy(delta, k).start()

    for load in loads[1:]:
        load.wait()
    per_row = cols // TILE_COLS
    own, cell_no = owner[...], cell[...]
    table = jnp.concatenate(
        [
            (target[...] * (rows // TILE_ROWS) + own // per_row).astype(F32),
            (own % per_row).astype(F32),
            net_e[...].astype(F32),
            weight[...],
            net_p[...].astype(F32),
            (cell_no // CELL_DEV).astype(F32),
            (cell_no % CELL_DEV).astype(F32),
            jnp.zeros_like(weight[...]),
        ],
        axis=0,
    )
    columns = jnp.transpose(table)
    entries = table.shape[1]
    net_e_col, wpin_col, net_p_col = columns[:, 2:3], columns[:, 3:4], columns[:, 4:5]
    strength = jnp.sum(
        jnp.where(net_p_col == table[2:3, :], wpin_col, 0.0), axis=0, keepdims=True
    )
    src_j = lax.broadcasted_iota(jnp.int32, (LANES, TILE_ROWS * LANES), 0)
    dst_j = lax.broadcasted_iota(jnp.int32, (LANES, TILE_ROWS * LANES), 1)
    pick = src_j == (dst_j // LANES) * TILE_COLS + dst_j % TILE_COLS
    spread = jnp.dot(
        frac[...], jnp.where(pick, 1.0, 0.0).astype(BF16), preferred_element_type=F32
    )
    wide = lax.broadcasted_iota(jnp.int32, (1, TILE_ROWS * LANES), 1) % LANES
    block = (wide + ci * own_cols - margin + TILE_COLS * LANES) // TILE_COLS - LANES
    fmask[...] = jnp.where(columns[:, 1:2] == block.astype(F32), spread, 0.0).astype(BF16)
    pad_blocks = HALO // TILE_ROWS
    blocks = dbuf.shape[0] // TILE_ROWS
    block_row = lax.broadcasted_iota(jnp.int32, (blocks, entries), 0).astype(F32)
    placed = jnp.where(block_row == table[0:1, :] + float(pad_blocks), strength, 0.0)
    left = jnp.concatenate(split(placed, 2), axis=0)
    partial = jnp.dot(left, fmask[...], preferred_element_type=F32)
    partial = partial[:blocks] + partial[blocks:]
    for i in range(TILE_ROWS):
        dbuf[pl.ds(i, blocks, stride=TILE_ROWS), :] = partial[:, i * LANES : (i + 1) * LANES]
    dsend[...] = dbuf[...].astype(BF16)

    def demand_copy(step):
        to = lax.rem(ti + step, tiles)
        return pltpu.make_async_remote_copy(
            src_ref=dsend.at[pl.ds(pl.multiple_of(to * rows, rows), in_rows)],
            dst_ref=drecv.at[step],
            send_sem=dsend_sem.at[step], recv_sem=drecv_sem.at[step],
            device_id=(to, ci), device_id_type=MESH,
        )

    def each(lo, hi, fn):
        def body(step, carry):
            fn(step)
            return carry
        lax.fori_loop(lo, hi, body, 0)

    each(1, tiles, lambda s: demand_copy(s).start())

    lift_row = lift[...]
    lift_col = jnp.transpose(jnp.broadcast_to(lift_row, (LANES, chan)))
    for u in range(3):
        for v in range(3):
            at_v, at_u = slice(v * chan, (v + 1) * chan), slice(u * chan, (u + 1) * chan)
            wm1[at_v, at_u] = jnp.transpose(w4[u, v].astype(F32)).astype(BF16)
            wm2[at_v, at_u] = jnp.transpose(w8[u, v].astype(F32)).astype(BF16)
            wm3[at_v, at_u] = w8[2 - u, 2 - v]
    taps = []
    for v in range(3):
        taps.append(
            jnp.concatenate(
                [
                    jnp.sum(
                        w4[2 - u, 2 - v].astype(F32) * lift_col[:, :chan], axis=0, keepdims=True
                    )
                    for u in range(3)
                ],
                axis=1,
            )
        )
    tap_rows = jnp.concatenate(taps + [jnp.zeros((5, 3 * chan), F32)], axis=0)
    hi, mid, low_part = [p.astype(F32) for p in split(tap_rows, 3)]
    wm4[...] = jnp.concatenate(
        [hi, mid, low_part, jnp.zeros((8, 3 * chan), F32)], axis=0
    ).astype(BF16)

    each(1, tiles, lambda s: demand_copy(s).wait())
    total = dsend[pl.ds(pl.multiple_of(ti * rows, rows), in_rows), :].astype(F32)
    total = lax.fori_loop(1, tiles, lambda s, t: t + drecv[s].astype(F32), total)
    demand[...] = total

    for delta, k in order:
        if delta == 0:
            if k == 0:
                feat_copy(delta, k).wait()
            else:
                feat_copy(delta, k).wait_send()
                feat_arrival(delta, k).wait_recv()
        else:
            @pl.when((ti + delta >= 0) & (ti + delta < tiles))
            def _(delta=delta, k=k):
                feat_copy(delta, k).wait_send()

            @pl.when((ti - delta >= 0) & (ti - delta < tiles))
            def _(delta=delta, k=k):
                feat_arrival(delta, k).wait_recv()

    height = rows * tiles
    top = ti * rows

    def in_map(row):
        return (row >= 0) & (row < height)

    def fill(g, carry):
        at = g * GROUP
        ok = in_map(top - HALO + at)

        @pl.when(ok)
        def _():
            for j in range(GROUP):
                add = lift_col * demand[pl.ds(at + j, 1), :]
                inp[at + j] = (gath[at + j].astype(F32) + add).astype(BF16)

        @pl.when(jnp.logical_not(ok))
        def _():
            for j in range(GROUP):
                inp[at + j] = jnp.zeros((chan, LANES), BF16)

        return carry

    lax.fori_loop(0, in_rows // GROUP, fill, 0)

    col = lane + ci * own_cols - margin
    col_ok = ((col >= 0) & (col < cols)).astype(F32)

    def gathered(ref, at, dilation):
        return jnp.concatenate(
            [
                jnp.concatenate([ref[at + j + u * dilation] for u in range(3)], axis=0)
                for j in range(GROUP)
            ],
            axis=1,
        )

    def conv(ref, at, weights, dilation):
        result = jnp.dot(weights[...], gathered(ref, at, dilation), preferred_element_type=F32)
        parts = []
        for j in range(GROUP):
            one = result[:, j * LANES : (j + 1) * LANES]
            parts.append(
                one[chan : 2 * chan]
                + pltpu.roll(one[:chan], dilation, 1)
                + pltpu.roll(one[2 * chan :], LANES - dilation, 1)
            )
        return parts

    def keep_of(row):
        return col_ok * in_map(row).astype(F32)

    def first(g, carry):
        at = g * GROUP
        keep = keep_of(top - 20 + at)
        for j, value in enumerate(conv(inp, at, wm1, 4)):
            pre[at + j] = value
            hid[at + j] = (value * jax.nn.sigmoid(value) * keep).astype(BF16)
        return carry

    def second(g, carry):
        at = g * GROUP
        keep = keep_of(top - 12 + at)
        for j, value in enumerate(conv(hid, at, wm2, 8)):
            sec[at + j] = (jax.nn.sigmoid(value) * keep).astype(BF16)
        return carry

    def third(g, carry):
        at = g * GROUP
        keep = keep_of(top - 4 + at)
        for j, value in enumerate(conv(sec, at, wm3, 8)):
            p = pre[at + j + 16]
            s = jax.nn.sigmoid(p)
            gpre[at + j] = (value * s * (1.0 + p * (1.0 - s)) * keep).astype(BF16)
        return carry

    lax.fori_loop(0, (rows + 40) // GROUP, first, 0)
    lax.fori_loop(0, (rows + 24) // GROUP, second, 0)
    lax.fori_loop(0, (rows + 8) // GROUP, third, 0)

    owned = ((lane >= margin) & (lane < margin + own_cols)).astype(F32)
    for g in range(rows // GROUP):
        at = g * GROUP
        result = jnp.dot(wm4[...], gathered(gpre, at, 4), preferred_element_type=F32)
        result = result[0:8] + result[8:16] + result[16:24]
        for j in range(GROUP):
            one = result[:, j * LANES : (j + 1) * LANES]
            line = (
                one[1:2]
                + pltpu.roll(one, 4, 1)[0:1]
                + pltpu.roll(one, LANES - 4, 1)[2:3]
            )
            gown[at + j : at + j + 1, :] = line * owned

    def grad_copy(step):
        to = lax.rem(ti + step, tiles)
        return pltpu.make_async_remote_copy(
            src_ref=gown, dst_ref=gall.at[pl.ds(pl.multiple_of(ti * rows, rows), rows)],
            send_sem=gsend_sem.at[step], recv_sem=grecv_sem.at[step],
            device_id=(to, ci), device_id_type=MESH,
        )

    def grad_arrival(step):
        come = lax.rem(ti + tiles - step, tiles)
        dst = gall.at[pl.ds(pl.multiple_of(come * rows, rows), rows)]
        return pltpu.make_async_remote_copy(
            src_ref=gown, dst_ref=dst,
            send_sem=gsend_sem.at[step], recv_sem=grecv_sem.at[step],
            device_id=(lax.rem(ti + step, tiles), ci), device_id_type=MESH,
        )

    each(1, tiles, lambda s: grad_copy(s).start())
    mine = pltpu.make_async_copy(
        gown, gall.at[pl.ds(pl.multiple_of(ti * rows, rows), rows)], gown_sem
    )
    mine.start()
    map_blocks = height // TILE_ROWS
    block_lane = lax.broadcasted_iota(jnp.int32, (entries, map_blocks), 1).astype(F32)
    block_hot = jnp.where(columns[:, 0:1] == block_lane, 1.0, 0.0).astype(BF16)
    mine.wait()
    each(1, tiles, lambda s: grad_copy(s).wait_send())
    each(1, tiles, lambda s: grad_arrival(s).wait_recv())

    entry_sum = jnp.zeros((entries, LANES), F32)
    for i in range(TILE_ROWS):
        grads = gall[pl.ds(i, map_blocks, stride=TILE_ROWS), :]
        high, low_ = split(grads, 2)
        rows_of = jnp.dot(block_hot, high, preferred_element_type=F32)
        rows_of = rows_of + jnp.dot(block_hot, low_, preferred_element_type=F32)
        entry_sum = entry_sum + rows_of * fmask[:, i * LANES : (i + 1) * LANES].astype(F32)
    entry_grad = jnp.sum(entry_sum, axis=1, keepdims=True)
    pin_grad = jnp.sum(
        jnp.where(net_e_col == table[4:5, :], entry_grad, 0.0), axis=0, keepdims=True
    )
    dest_rows = max(8, tiles)
    dest_row = lax.broadcasted_iota(jnp.int32, (dest_rows, entries), 0).astype(F32)
    cell_row = lax.broadcasted_iota(jnp.int32, (LANES, entries), 0).astype(F32)
    by_dest = jnp.where(dest_row == table[5:6, :], pin_grad, 0.0)
    by_cell = jnp.where(cell_row == table[6:7, :], 1.0, 0.0).astype(BF16)
    pieces = jnp.concatenate([p.astype(F32) for p in split(by_dest, 3)], axis=0).astype(BF16)
    cells = lax.dot_general(
        pieces, by_cell, (((1,), (1,)), ((), ())), preferred_element_type=F32
    )
    cells = cells[:dest_rows] + cells[dest_rows : 2 * dest_rows] + cells[2 * dest_rows :]
    for t in range(tiles):
        csend[t] = cells[t : t + 1, :]

    def cell_copy(step):
        to = peer(step)
        return pltpu.make_async_remote_copy(
            src_ref=csend.at[to[0]], dst_ref=crecv.at[step],
            send_sem=csend_sem.at[step], recv_sem=crecv_sem.at[step],
            device_id=to, device_id_type=MESH,
        )

    each(1, others + 1, lambda s: cell_copy(s).start())
    each(1, others + 1, lambda s: cell_copy(s).wait())
    out[...] = lax.fori_loop(1, others + 1, lambda s, t: t + crecv[s], csend[ti])


def solution(mesh):
    tiles, chans = mesh.shape["tile"], mesh.shape["chan"]

    def local(
        feat, lift, w4, w8, frac, target, owner, net_e, weight, net_p, cell,
    ):
        rows, chan_own, cols = feat.shape
        chan = chan_own * chans
        entries = frac.shape[0]
        pins = weight.shape[0]
        in_rows = rows + 2 * HALO
        reach = -(-HALO // rows)
        height = rows * tiles
        blocks = -(-(height + 2 * HALO) // (8 * TILE_ROWS)) * 8
        vm = pltpu.VMEM
        dma = pltpu.SemaphoreType.DMA
        result = pl.pallas_call(
            functools.partial(kernel, tiles, chans),
            out_shape=jax.ShapeDtypeStruct((1, LANES), F32),
            in_specs=[pl.BlockSpec(memory_space=pltpu.HBM)] * 11,
            out_specs=pl.BlockSpec(memory_space=pltpu.VMEM),
            scratch_shapes=[
                vm(feat.shape, BF16),
                vm((1, chan), F32),
                vm(w4.shape, BF16),
                vm(w8.shape, BF16),
                vm(frac.shape, BF16),
                vm((1, entries), jnp.int32),
                vm((1, entries), jnp.int32),
                vm((1, entries), jnp.int32),
                vm((1, pins), F32),
                vm((1, pins), jnp.int32),
                vm((1, pins), jnp.int32),
                dma((11,)),
                vm((chans, rows, chan_own, LANES), BF16),
                vm((in_rows, chan, LANES), BF16),
                vm((in_rows, chan, LANES), BF16),
                vm((rows + 40, chan, LANES), F32),
                vm((rows + 40, chan, LANES), BF16),
                vm((rows + 24, chan, LANES), BF16),
                vm((rows + 8, chan, LANES), BF16),
                vm((3 * chan, 3 * chan), BF16),
                vm((3 * chan, 3 * chan), BF16),
                vm((3 * chan, 3 * chan), BF16),
                vm((32, 3 * chan), BF16),
                vm((entries, TILE_ROWS * LANES), BF16),
                vm((blocks * TILE_ROWS, LANES), F32),
                vm((blocks * TILE_ROWS, LANES), BF16),
                vm((tiles, in_rows, LANES), BF16),
                vm((in_rows, LANES), F32),
                vm((rows, LANES), F32),
                vm((height, LANES), F32),
                vm((tiles, 1, LANES), F32),
                vm((tiles * chans, 1, LANES), F32),
                dma((2 * reach + 1, chans)),
                dma((2 * reach + 1, chans)),
                dma(()),
                dma((tiles,)),
                dma((tiles,)),
                dma((tiles,)),
                dma((tiles,)),
                dma(()),
                dma((tiles * chans,)),
                dma((tiles * chans,)),
            ],
            compiler_params=pltpu.CompilerParams(collective_id=0, has_side_effects=True),
        )(
            feat, lift.reshape(1, chan), w4, w8, frac, target.reshape(1, entries),
            owner.reshape(1, entries), net_e.reshape(1, entries), weight.reshape(1, pins),
            net_p.reshape(1, pins), cell.reshape(1, pins),
        )
        return result[0, :CELL_DEV]

    in_specs = (
        P("tile", "chan", None), P(), P(), P(),
        P("tile", None), P("tile", None),
        P("tile"), P("tile"), P("tile"), P("tile"), P("tile"),
    )
    return jax.shard_map(
        local, mesh=mesh, in_specs=in_specs, out_specs=P("tile"), check_vma=False
    )
```

```python
import functools

import jax
import jax.numpy as jnp
from jax import lax
from jax.experimental import pallas as pl
from jax.experimental.pallas import tpu as pltpu
from jax.sharding import PartitionSpec as P

MESH = pl.DeviceIdType.MESH
CELL_DEV = 64
TILE_ROWS = 8
TILE_COLS = 16
LANES = 128
HALO = 24
GROUP = 4
F32 = jnp.float32
BF16 = jnp.bfloat16


def split(x, terms):
    parts = []
    for _ in range(terms):
        part = x.astype(BF16)
        parts.append(part)
        x = x - part.astype(F32)
    return parts


def kernel(
    tiles, chans,
    feat_in, lift_in, w4_in, w8_in, frac_in, target_in, owner_in, net_e_in, weight_in, net_p_in,
    cell_in,
    out,
    feat, lift, w4, w8, frac, target, owner, net_e, weight, net_p, cell, load_sem,
    win, gath, inp, pre, hid, sec, gpre, wm1, wm2, wm3, wm4,
    fmask, block_hot, same_net, by_dest, by_cell, dbuf, dsend, drecv, demand, gown, gall, csend, crecv,
    fsend_sem, frecv_sem, own_sem, dsend_sem, drecv_sem, gsend_sem, grecv_sem, gown_sem,
    csend_sem, crecv_sem,
):
    ti = lax.axis_index("tile")
    ci = lax.axis_index("chan")
    rows, chan_own, cols = feat.shape
    chan = chan_own * chans
    own_cols = cols // chans
    margin = (LANES - own_cols) // 2
    reach = -(-HALO // rows)
    in_rows = rows + 2 * HALO
    others = tiles * chans - 1

    loads = [
        pltpu.make_async_copy(src, dst, load_sem.at[n])
        for n, (src, dst) in enumerate(
            [
                (feat_in, feat), (target_in, target), (owner_in, owner), (net_e_in, net_e),
                (weight_in, weight), (net_p_in, net_p), (frac_in, frac), (lift_in, lift),
                (cell_in, cell), (w4_in, w4), (w8_in, w8),
            ]
        )
    ]
    for load in loads:
        load.start()

    barrier = pltpu.get_barrier_semaphore()

    def wrap(number, count):
        return jnp.where(number >= count, number - count, number)

    def each(lo, hi, fn):
        if hi - lo <= 32:
            for step in range(lo, hi):
                fn(step)
        else:
            def body(step, carry):
                fn(step)
                return carry
            lax.fori_loop(lo, hi, body, 0)

    def each_peer(fn):
        def along(back):
            hop = tiles - 1 - back
            for turn in range(chans):
                fn(hop * chans + turn, (wrap(ti + hop, tiles), wrap(ci + turn, chans)))
        each(0, tiles - 1, along)
        for turn in range(1, chans):
            fn(turn, (ti, wrap(ci + turn, chans)))

    each_peer(
        lambda n, who: pl.semaphore_signal(barrier, inc=1, device_id=who, device_id_type=MESH)
    )

    loads[0].wait()

    flat = feat[...].astype(F32).reshape(rows * chan_own, cols)
    lane = lax.broadcasted_iota(jnp.int32, (1, LANES), 1)
    for k in range(chans):
        first = k * own_cols - margin
        turned = pltpu.roll(flat, (-first) % cols, 1)[:, :LANES]
        inside = (lane + first >= 0) & (lane + first < cols)
        win[k] = jnp.where(inside, turned, 0.0).astype(BF16).reshape(rows, chan_own, LANES)

    pl.semaphore_wait(barrier, others)

    def spans(delta):
        start = HALO - rows * delta
        low = max(0, -start)
        high = min(rows, in_rows - start)
        return low, high - low, start + low

    def feat_copy(delta, k):
        low, count, at = spans(delta)
        to = wrap(ci + k, chans)
        src = win.at[to, pl.ds(low, count)]
        dst = gath.at[pl.ds(at, count), pl.ds(pl.multiple_of(ci * chan_own, chan_own), chan_own)]
        if delta == 0 and k == 0:
            return pltpu.make_async_copy(src, dst, own_sem)
        return pltpu.make_async_remote_copy(
            src_ref=src, dst_ref=dst,
            send_sem=fsend_sem.at[delta + reach, k], recv_sem=frecv_sem.at[delta + reach, k],
            device_id=(ti + delta, to), device_id_type=MESH,
        )

    def feat_arrival(delta, k):
        low, count, at = spans(delta)
        come = wrap(ci + chans - k, chans)
        dst = gath.at[pl.ds(at, count), pl.ds(pl.multiple_of(come * chan_own, chan_own), chan_own)]
        return pltpu.make_async_remote_copy(
            src_ref=dst, dst_ref=dst,
            send_sem=fsend_sem.at[delta + reach, k], recv_sem=frecv_sem.at[delta + reach, k],
            device_id=(ti, wrap(ci + 1, chans)), device_id_type=MESH,
        )

    stages = [[0]] + [[d] if abs(d) == 1 else [d, -d] for d in (1, -1, *range(2, reach + 1))]
    for delta in sum(stages, []):
        for k in range(chans):
            if delta == 0:
                feat_copy(delta, k).start()
            else:
                @pl.when((ti + delta >= 0) & (ti + delta < tiles))
                def _(delta=delta, k=k):
                    feat_copy(delta, k).start()

    for delta in sum(stages[1:], []):
        @pl.when((ti - delta < 0) | (ti - delta >= tiles))
        def _(delta=delta):
            low, count, at = spans(delta)
            gath[at : at + count] = jnp.zeros((count, chan, LANES), BF16)

    for load in loads[1:]:
        load.wait()
    per_row = cols // TILE_COLS
    own, cell_no = owner[...], cell[...]
    table = jnp.concatenate(
        [
            (target[...] * (rows // TILE_ROWS) + own // per_row).astype(F32),
            (own % per_row).astype(F32),
            net_e[...].astype(F32),
            weight[...],
            net_p[...].astype(F32),
            (cell_no // CELL_DEV).astype(F32),
            (cell_no % CELL_DEV).astype(F32),
            jnp.zeros_like(weight[...]),
        ],
        axis=0,
    )
    columns = jnp.transpose(table)
    entries = table.shape[1]
    net_e_col, wpin_col, net_p_col = columns[:, 2:3], columns[:, 3:4], columns[:, 4:5]
    strength = jnp.sum(
        jnp.where(net_p_col == table[2:3, :], wpin_col, 0.0), axis=0, keepdims=True
    )
    src_j = lax.broadcasted_iota(jnp.int32, (LANES, TILE_ROWS * LANES), 0)
    dst_j = lax.broadcasted_iota(jnp.int32, (LANES, TILE_ROWS * LANES), 1)
    pick = src_j == (dst_j // LANES) * TILE_COLS + dst_j % TILE_COLS
    spread = jnp.dot(
        frac[...], jnp.where(pick, 1.0, 0.0).astype(BF16), preferred_element_type=F32
    )
    wide = lax.broadcasted_iota(jnp.int32, (1, TILE_ROWS * LANES), 1) % LANES
    block = (wide + ci * own_cols - margin + TILE_COLS * LANES) // TILE_COLS - LANES
    fmask[...] = jnp.where(columns[:, 1:2] == block.astype(F32), spread, 0.0).astype(BF16)
    pad_blocks = HALO // TILE_ROWS
    blocks = dbuf.shape[0] // TILE_ROWS
    block_row = lax.broadcasted_iota(jnp.int32, (blocks, entries), 0).astype(F32)
    placed = jnp.where(block_row == table[0:1, :] + float(pad_blocks), strength, 0.0)
    left = jnp.concatenate(split(placed, 2), axis=0)
    partial = jnp.dot(left, fmask[...], preferred_element_type=F32)
    partial = partial[:blocks] + partial[blocks:]
    for i in range(TILE_ROWS):
        dbuf[pl.ds(i, blocks, stride=TILE_ROWS), :] = partial[:, i * LANES : (i + 1) * LANES]
    dsend[...] = dbuf[...].astype(BF16)

    def demand_copy(step):
        to = wrap(ti + step, tiles)
        return pltpu.make_async_remote_copy(
            src_ref=dsend.at[pl.ds(pl.multiple_of(to * rows, rows), in_rows)],
            dst_ref=drecv.at[step],
            send_sem=dsend_sem.at[step], recv_sem=drecv_sem.at[step],
            device_id=(to, ci), device_id_type=MESH,
        )

    each(1, tiles, lambda s: demand_copy(s).start())

    lift_row = lift[...]
    lift_col = jnp.transpose(jnp.broadcast_to(lift_row, (LANES, chan)))
    for u in range(3):
        for v in range(3):
            at_v, at_u = slice(v * chan, (v + 1) * chan), slice(u * chan, (u + 1) * chan)
            wm1[at_v, at_u] = jnp.transpose(w4[u, v].astype(F32)).astype(BF16)
            wm2[at_v, at_u] = jnp.transpose(w8[u, v].astype(F32)).astype(BF16)
            wm3[at_v, at_u] = w8[2 - u, 2 - v]
    taps = []
    for v in range(3):
        taps.append(
            jnp.concatenate(
                [
                    jnp.sum(
                        w4[2 - u, 2 - v].astype(F32) * lift_col[:, :chan], axis=0, keepdims=True
                    )
                    for u in range(3)
                ],
                axis=1,
            )
        )
    tap_rows = jnp.concatenate(taps + [jnp.zeros((5, 3 * chan), F32)], axis=0)
    hi, mid, low_part = [p.astype(F32) for p in split(tap_rows, 3)]
    wm4[...] = jnp.concatenate(
        [hi, mid, low_part, jnp.zeros((8, 3 * chan), F32)], axis=0
    ).astype(BF16)

    map_blocks = rows * tiles // TILE_ROWS
    block_lane = lax.broadcasted_iota(jnp.int32, (entries, map_blocks), 1).astype(F32)
    block_hot[...] = jnp.where(columns[:, 0:1] == block_lane, 1.0, 0.0).astype(BF16)
    same_net[...] = jnp.where(net_e_col == table[4:5, :], 1.0, 0.0)
    dest_rows = max(8, tiles)
    dest_row = lax.broadcasted_iota(jnp.int32, (dest_rows, entries), 0).astype(F32)
    cell_row = lax.broadcasted_iota(jnp.int32, (LANES, entries), 0).astype(F32)
    by_dest[...] = jnp.where(dest_row == table[5:6, :], 1.0, 0.0)
    by_cell[...] = jnp.where(cell_row == table[6:7, :], 1.0, 0.0).astype(BF16)

    each(1, tiles, lambda s: demand_copy(s).wait())
    total = dsend[pl.ds(pl.multiple_of(ti * rows, rows), in_rows), :].astype(F32)
    total = lax.fori_loop(1, tiles, lambda s, t: t + drecv[s].astype(F32), total)
    demand[...] = total

    def feat_wait(delta):
        if delta == 0:
            feat_copy(delta, 0).wait()
            for k in range(1, chans):
                feat_arrival(delta, k).wait_recv()
        else:
            @pl.when((ti - delta >= 0) & (ti - delta < tiles))
            def _():
                for k in range(chans):
                    feat_arrival(delta, k).wait_recv()

    height = rows * tiles
    top = ti * rows

    def in_map(row):
        return (row >= 0) & (row < height)

    def fill(at):
        for j in range(at, at + GROUP):
            add = lift_col * demand[j : j + 1, :]
            inp[j] = (gath[j].astype(F32) + add).astype(BF16)

    col = lane + ci * own_cols - margin
    col_ok = ((col >= 0) & (col < cols)).astype(F32)

    def gathered(ref, at, dilation):
        return jnp.concatenate(
            [
                jnp.concatenate([ref[at + j + u * dilation] for u in range(3)], axis=0)
                for j in range(GROUP)
            ],
            axis=1,
        )

    def conv(ref, at, weights, dilation):
        result = jnp.dot(weights[...], gathered(ref, at, dilation), preferred_element_type=F32)
        parts = []
        for j in range(GROUP):
            one = result[:, j * LANES : (j + 1) * LANES]
            parts.append(
                one[chan : 2 * chan]
                + pltpu.roll(one[:chan], dilation, 1)
                + pltpu.roll(one[2 * chan :], LANES - dilation, 1)
            )
        return parts

    def keep_of(row):
        return col_ok * in_map(row).astype(F32)

    def first(at):
        keep = keep_of(top - 20 + at)
        for j, value in enumerate(conv(inp, at, wm1, 4)):
            pre[at + j] = value
            hid[at + j] = (value * jax.nn.sigmoid(value) * keep).astype(BF16)

    def second(at):
        keep = keep_of(top - 12 + at)
        for j, value in enumerate(conv(hid, at, wm2, 8)):
            sec[at + j] = (jax.nn.sigmoid(value) * keep).astype(BF16)

    def third(at):
        keep = keep_of(top - 4 + at)
        for j, value in enumerate(conv(sec, at, wm3, 8)):
            p = pre[at + j + 16]
            s = jax.nn.sigmoid(p)
            gpre[at + j] = (value * s * (1.0 + p * (1.0 - s)) * keep).astype(BF16)

    here, done = set(), set()
    for stage in stages:
        fresh = set()
        for delta in stage:
            feat_wait(delta)
            low, count, at = spans(delta)
            fresh |= set(range(at, at + count))
        here |= fresh
        for at in range(0, in_rows, GROUP):
            if at in fresh:
                fill(at)
        for at in range(0, rows + 40, GROUP):
            if at not in done and all(at + j in here for j in range(GROUP + 8)):
                done.add(at)
                first(at)
    for at in range(0, rows + 24, GROUP):
        second(at)
    for at in range(0, rows + 8, GROUP):
        third(at)

    owned = ((lane >= margin) & (lane < margin + own_cols)).astype(F32)
    for g in range(rows // GROUP):
        at = g * GROUP
        result = jnp.dot(wm4[...], gathered(gpre, at, 4), preferred_element_type=F32)
        result = result[0:8] + result[8:16] + result[16:24]
        for j in range(GROUP):
            one = result[:, j * LANES : (j + 1) * LANES]
            line = (
                one[1:2]
                + pltpu.roll(one, 4, 1)[0:1]
                + pltpu.roll(one, LANES - 4, 1)[2:3]
            )
            gown[at + j : at + j + 1, :] = line * owned

    def grad_copy(step):
        to = wrap(ti + step, tiles)
        return pltpu.make_async_remote_copy(
            src_ref=gown, dst_ref=gall.at[pl.ds(pl.multiple_of(ti * rows, rows), rows)],
            send_sem=gsend_sem.at[step], recv_sem=grecv_sem.at[step],
            device_id=(to, ci), device_id_type=MESH,
        )

    def grad_arrival(step):
        come = wrap(ti + tiles - step, tiles)
        dst = gall.at[pl.ds(pl.multiple_of(come * rows, rows), rows)]
        return pltpu.make_async_remote_copy(
            src_ref=gown, dst_ref=dst,
            send_sem=gsend_sem.at[step], recv_sem=grecv_sem.at[step],
            device_id=(wrap(ti + step, tiles), ci), device_id_type=MESH,
        )

    each(1, tiles, lambda s: grad_copy(s).start())
    mine = pltpu.make_async_copy(
        gown, gall.at[pl.ds(pl.multiple_of(ti * rows, rows), rows)], gown_sem
    )
    mine.start()
    mine.wait()
    each(1, tiles, lambda s: grad_arrival(s).wait_recv())

    entry_sum = jnp.zeros((entries, LANES), F32)
    for i in range(TILE_ROWS):
        grads = gall[pl.ds(i, map_blocks, stride=TILE_ROWS), :]
        high, low_ = split(grads, 2)
        rows_of = jnp.dot(block_hot[...], high, preferred_element_type=F32)
        rows_of = rows_of + jnp.dot(block_hot[...], low_, preferred_element_type=F32)
        entry_sum = entry_sum + rows_of * fmask[:, i * LANES : (i + 1) * LANES].astype(F32)
    entry_grad = jnp.sum(entry_sum, axis=1, keepdims=True)
    pin_grad = jnp.sum(same_net[...] * entry_grad, axis=0, keepdims=True)
    pieces = jnp.concatenate([p.astype(F32) for p in split(by_dest[...] * pin_grad, 3)], axis=0).astype(BF16)
    cells = lax.dot_general(
        pieces, by_cell[...], (((1,), (1,)), ((), ())), preferred_element_type=F32
    )
    cells = cells[:dest_rows] + cells[dest_rows : 2 * dest_rows] + cells[2 * dest_rows :]
    for t in range(tiles):
        csend[t] = cells[t : t + 1, :]

    def cell_copy(step, to):
        return pltpu.make_async_remote_copy(
            src_ref=csend.at[to[0]], dst_ref=crecv.at[step],
            send_sem=csend_sem, recv_sem=crecv_sem,
            device_id=to, device_id_type=MESH,
        )

    each_peer(lambda n, who: cell_copy(n, who).start())

    for delta in sum(stages, []):
        for k in range(chans):
            if delta == 0:
                if k:
                    feat_copy(delta, k).wait_send()
            else:
                @pl.when((ti + delta >= 0) & (ti + delta < tiles))
                def _(delta=delta, k=k):
                    feat_copy(delta, k).wait_send()
    each(1, tiles, lambda s: grad_copy(s).wait_send())
    arrived = crecv.at[pl.ds(1, others)]
    pltpu.make_async_remote_copy(
        src_ref=arrived, dst_ref=arrived, send_sem=csend_sem, recv_sem=crecv_sem,
        device_id=(ti, wrap(ci + 1, chans)), device_id_type=MESH,
    ).wait()
    out[...] = csend[ti] + jnp.sum(crecv[1:], axis=0)


def solution(mesh):
    tiles, chans = mesh.shape["tile"], mesh.shape["chan"]

    def local(
        feat, lift, w4, w8, frac, target, owner, net_e, weight, net_p, cell,
    ):
        rows, chan_own, cols = feat.shape
        chan = chan_own * chans
        entries = frac.shape[0]
        pins = weight.shape[0]
        in_rows = rows + 2 * HALO
        reach = -(-HALO // rows)
        height = rows * tiles
        blocks = -(-(height + 2 * HALO) // (8 * TILE_ROWS)) * 8
        vm = pltpu.VMEM
        dma = pltpu.SemaphoreType.DMA
        result = pl.pallas_call(
            functools.partial(kernel, tiles, chans),
            out_shape=jax.ShapeDtypeStruct((1, LANES), F32),
            in_specs=[pl.BlockSpec(memory_space=pltpu.HBM)] * 11,
            out_specs=pl.BlockSpec(memory_space=pltpu.VMEM),
            scratch_shapes=[
                vm(feat.shape, BF16),
                vm((1, chan), F32),
                vm(w4.shape, BF16),
                vm(w8.shape, BF16),
                vm(frac.shape, BF16),
                vm((1, entries), jnp.int32),
                vm((1, entries), jnp.int32),
                vm((1, entries), jnp.int32),
                vm((1, pins), F32),
                vm((1, pins), jnp.int32),
                vm((1, pins), jnp.int32),
                dma((11,)),
                vm((chans, rows, chan_own, LANES), BF16),
                vm((in_rows, chan, LANES), BF16),
                vm((in_rows, chan, LANES), BF16),
                vm((rows + 40, chan, LANES), F32),
                vm((rows + 40, chan, LANES), BF16),
                vm((rows + 24, chan, LANES), BF16),
                vm((rows + 8, chan, LANES), BF16),
                vm((3 * chan, 3 * chan), BF16),
                vm((3 * chan, 3 * chan), BF16),
                vm((3 * chan, 3 * chan), BF16),
                vm((32, 3 * chan), BF16),
                vm((entries, TILE_ROWS * LANES), BF16),
                vm((entries, height // TILE_ROWS), BF16),
                vm((entries, pins), F32),
                vm((max(8, tiles), pins), F32),
                vm((LANES, pins), BF16),
                vm((blocks * TILE_ROWS, LANES), F32),
                vm((blocks * TILE_ROWS, LANES), BF16),
                vm((tiles, in_rows, LANES), BF16),
                vm((in_rows, LANES), F32),
                vm((rows, LANES), F32),
                vm((height, LANES), F32),
                vm((tiles, 1, LANES), F32),
                vm((tiles * chans, 1, LANES), F32),
                dma((2 * reach + 1, chans)),
                dma((2 * reach + 1, chans)),
                dma(()),
                dma((tiles,)),
                dma((tiles,)),
                dma((tiles,)),
                dma((tiles,)),
                dma(()),
                dma(()),
                dma(()),
            ],
            compiler_params=pltpu.CompilerParams(collective_id=0, has_side_effects=True),
        )(
            feat, lift.reshape(1, chan), w4, w8, frac, target.reshape(1, entries),
            owner.reshape(1, entries), net_e.reshape(1, entries), weight.reshape(1, pins),
            net_p.reshape(1, pins), cell.reshape(1, pins),
        )
        return result[0, :CELL_DEV]

    in_specs = (
        P("tile", "chan", None), P(), P(), P(),
        P("tile", None), P("tile", None),
        P("tile"), P("tile"), P("tile"), P("tile"), P("tile"),
    )
    return jax.shard_map(
        local, mesh=mesh, in_specs=in_specs, out_specs=P("tile"), check_vma=False
    )
```

```python
import functools

import jax
import jax.numpy as jnp
from jax import lax
from jax.experimental import pallas as pl
from jax.experimental.pallas import tpu as pltpu
from jax.sharding import PartitionSpec as P

MESH = pl.DeviceIdType.MESH
CELL_DEV = 64
TILE_ROWS = 8
TILE_COLS = 16
LANES = 128
HALO = 24
GROUP = 4
F32 = jnp.float32
BF16 = jnp.bfloat16


def split(x, terms):
    parts = []
    for _ in range(terms):
        part = x.astype(BF16)
        parts.append(part)
        x = x - part.astype(F32)
    return parts


def kernel(
    tiles, chans,
    feat_in, lift_in, w4_in, w8_in, frac_in, target_in, owner_in, net_e_in, weight_in, net_p_in,
    cell_in,
    out,
    feat, lift, w4, w8, frac, target, owner, net_e, weight, net_p, cell, load_sem,
    win, gath, inp, pre, hid, sec, gpre, wm1, wm2, wm3, wm4,
    fmask, block_hot, same_net, by_dest, by_cell, dbuf, dsend, drecv, demand, gown, gall, csend, crecv,
    fsend_sem, frecv_sem, own_sem, dsend_sem, drecv_sem, gsend_sem, grecv_sem, gown_sem,
    csend_sem, crecv_sem,
):
    ti = lax.axis_index("tile")
    ci = lax.axis_index("chan")
    rows, chan_own, cols = feat.shape
    chan = chan_own * chans
    own_cols = cols // chans
    margin = (LANES - own_cols) // 2
    reach = -(-HALO // rows)
    in_rows = rows + 2 * HALO
    others = tiles * chans - 1

    loads = [
        pltpu.make_async_copy(src, dst, load_sem.at[n])
        for n, (src, dst) in enumerate(
            [
                (feat_in, feat), (target_in, target), (owner_in, owner), (net_e_in, net_e),
                (weight_in, weight), (net_p_in, net_p), (frac_in, frac), (lift_in, lift),
                (cell_in, cell), (w4_in, w4), (w8_in, w8),
            ]
        )
    ]
    for load in loads:
        load.start()

    barrier = pltpu.get_barrier_semaphore()

    def wrap(number, count):
        return jnp.where(number >= count, number - count, number)

    def each(lo, hi, fn):
        if hi - lo <= 32:
            for step in range(lo, hi):
                fn(step)
        else:
            def body(step, carry):
                fn(step)
                return carry
            lax.fori_loop(lo, hi, body, 0)

    def each_peer(fn):
        def along(back):
            hop = tiles - 1 - back
            for turn in range(chans):
                fn(hop * chans + turn, (wrap(ti + hop, tiles), wrap(ci + turn, chans)))
        each(0, tiles - 1, along)
        for turn in range(1, chans):
            fn(turn, (ti, wrap(ci + turn, chans)))

    each_peer(
        lambda n, who: pl.semaphore_signal(barrier, inc=1, device_id=who, device_id_type=MESH)
    )

    loads[0].wait()

    flat = feat[...].astype(F32).reshape(rows * chan_own, cols)
    lane = lax.broadcasted_iota(jnp.int32, (1, LANES), 1)
    for k in range(chans):
        first = k * own_cols - margin
        turned = pltpu.roll(flat, (-first) % cols, 1)[:, :LANES]
        inside = (lane + first >= 0) & (lane + first < cols)
        win[k] = jnp.where(inside, turned, 0.0).astype(BF16).reshape(rows, chan_own, LANES)

    def spans(delta):
        start = HALO - rows * delta
        low = max(0, -start)
        high = min(rows, in_rows - start)
        return low, high - low, start + low

    def feat_copy(delta, k):
        low, count, at = spans(delta)
        to = wrap(ci + k, chans)
        src = win.at[to, pl.ds(low, count)]
        dst = gath.at[pl.ds(at, count), pl.ds(pl.multiple_of(ci * chan_own, chan_own), chan_own)]
        if delta == 0 and k == 0:
            return pltpu.make_async_copy(src, dst, own_sem)
        return pltpu.make_async_remote_copy(
            src_ref=src, dst_ref=dst,
            send_sem=fsend_sem.at[delta + reach, k], recv_sem=frecv_sem.at[delta + reach, k],
            device_id=(ti + delta, to), device_id_type=MESH,
        )

    def feat_arrival(delta, k):
        low, count, at = spans(delta)
        come = wrap(ci + chans - k, chans)
        dst = gath.at[pl.ds(at, count), pl.ds(pl.multiple_of(come * chan_own, chan_own), chan_own)]
        return pltpu.make_async_remote_copy(
            src_ref=dst, dst_ref=dst,
            send_sem=fsend_sem.at[delta + reach, k], recv_sem=frecv_sem.at[delta + reach, k],
            device_id=(ti, wrap(ci + 1, chans)), device_id_type=MESH,
        )

    stages = [[0]] + [[d] if abs(d) == 1 else [d, -d] for d in (1, -1, *range(2, reach + 1))]
    for delta in sum(stages[1:], []):
        @pl.when((ti - delta < 0) | (ti - delta >= tiles))
        def _(delta=delta):
            low, count, at = spans(delta)
            gath[at : at + count] = jnp.zeros((count, chan, LANES), BF16)

    for load in loads[1:]:
        load.wait()
    per_row = cols // TILE_COLS
    own, cell_no = owner[...], cell[...]
    table = jnp.concatenate(
        [
            (target[...] * (rows // TILE_ROWS) + own // per_row).astype(F32),
            (own % per_row).astype(F32),
            net_e[...].astype(F32),
            weight[...],
            net_p[...].astype(F32),
            (cell_no // CELL_DEV).astype(F32),
            (cell_no % CELL_DEV).astype(F32),
            jnp.zeros_like(weight[...]),
        ],
        axis=0,
    )
    columns = jnp.transpose(table)
    entries = table.shape[1]
    net_e_col, wpin_col, net_p_col = columns[:, 2:3], columns[:, 3:4], columns[:, 4:5]
    strength = jnp.sum(
        jnp.where(net_p_col == table[2:3, :], wpin_col, 0.0), axis=0, keepdims=True
    )
    src_j = lax.broadcasted_iota(jnp.int32, (LANES, TILE_ROWS * LANES), 0)
    dst_j = lax.broadcasted_iota(jnp.int32, (LANES, TILE_ROWS * LANES), 1)
    pick = src_j == (dst_j // LANES) * TILE_COLS + dst_j % TILE_COLS
    spread = jnp.dot(
        frac[...], jnp.where(pick, 1.0, 0.0).astype(BF16), preferred_element_type=F32
    )
    wide = lax.broadcasted_iota(jnp.int32, (1, TILE_ROWS * LANES), 1) % LANES
    block = (wide + ci * own_cols - margin + TILE_COLS * LANES) // TILE_COLS - LANES
    fmask[...] = jnp.where(columns[:, 1:2] == block.astype(F32), spread, 0.0).astype(BF16)
    pad_blocks = HALO // TILE_ROWS
    blocks = dbuf.shape[0] // TILE_ROWS
    block_row = lax.broadcasted_iota(jnp.int32, (blocks, entries), 0).astype(F32)
    placed = jnp.where(block_row == table[0:1, :] + float(pad_blocks), strength, 0.0)
    left = jnp.concatenate(split(placed, 2), axis=0)
    partial = jnp.dot(left, fmask[...], preferred_element_type=F32)
    partial = partial[:blocks] + partial[blocks:]
    for i in range(TILE_ROWS):
        dbuf[pl.ds(i, blocks, stride=TILE_ROWS), :] = partial[:, i * LANES : (i + 1) * LANES]
    dsend[...] = dbuf[...].astype(BF16)

    def demand_copy(step):
        to = wrap(ti + step, tiles)
        return pltpu.make_async_remote_copy(
            src_ref=dsend.at[pl.ds(pl.multiple_of(to * rows, rows), in_rows)],
            dst_ref=drecv.at[step],
            send_sem=dsend_sem.at[step], recv_sem=drecv_sem.at[step],
            device_id=(to, ci), device_id_type=MESH,
        )

    lift_row = lift[...]
    lift_col = jnp.transpose(jnp.broadcast_to(lift_row, (LANES, chan)))
    for u in range(3):
        for v in range(3):
            at_v, at_u = slice(v * chan, (v + 1) * chan), slice(u * chan, (u + 1) * chan)
            wm1[at_v, at_u] = jnp.transpose(w4[u, v].astype(F32)).astype(BF16)
            wm2[at_v, at_u] = jnp.transpose(w8[u, v].astype(F32)).astype(BF16)
            wm3[at_v, at_u] = w8[2 - u, 2 - v]
    taps = []
    for v in range(3):
        taps.append(
            jnp.concatenate(
                [
                    jnp.sum(
                        w4[2 - u, 2 - v].astype(F32) * lift_col[:, :chan], axis=0, keepdims=True
                    )
                    for u in range(3)
                ],
                axis=1,
            )
        )
    tap_rows = jnp.concatenate(taps + [jnp.zeros((5, 3 * chan), F32)], axis=0)
    hi, mid, low_part = [p.astype(F32) for p in split(tap_rows, 3)]
    wm4[...] = jnp.concatenate(
        [hi, mid, low_part, jnp.zeros((8, 3 * chan), F32)], axis=0
    ).astype(BF16)

    map_blocks = rows * tiles // TILE_ROWS
    block_lane = lax.broadcasted_iota(jnp.int32, (entries, map_blocks), 1).astype(F32)
    block_hot[...] = jnp.where(columns[:, 0:1] == block_lane, 1.0, 0.0).astype(BF16)
    same_net[...] = jnp.where(net_e_col == table[4:5, :], 1.0, 0.0)
    dest_rows = max(8, tiles)
    dest_row = lax.broadcasted_iota(jnp.int32, (dest_rows, entries), 0).astype(F32)
    cell_row = lax.broadcasted_iota(jnp.int32, (LANES, entries), 0).astype(F32)
    by_dest[...] = jnp.where(dest_row == table[5:6, :], 1.0, 0.0)
    by_cell[...] = jnp.where(cell_row == table[6:7, :], 1.0, 0.0).astype(BF16)

    pl.semaphore_wait(barrier, others)

    each(1, tiles, lambda s: demand_copy(s).start())

    for delta in sum(stages, []):
        for k in range(chans):
            if delta == 0:
                feat_copy(delta, k).start()
            else:
                @pl.when((ti + delta >= 0) & (ti + delta < tiles))
                def _(delta=delta, k=k):
                    feat_copy(delta, k).start()

    each(1, tiles, lambda s: demand_copy(s).wait())
    total = dsend[pl.ds(pl.multiple_of(ti * rows, rows), in_rows), :].astype(F32)
    total = lax.fori_loop(1, tiles, lambda s, t: t + drecv[s].astype(F32), total)
    demand[...] = total

    def feat_wait(delta):
        if delta == 0:
            feat_copy(delta, 0).wait()
            for k in range(1, chans):
                feat_arrival(delta, k).wait_recv()
        else:
            @pl.when((ti - delta >= 0) & (ti - delta < tiles))
            def _():
                for k in range(chans):
                    feat_arrival(delta, k).wait_recv()

    height = rows * tiles
    top = ti * rows

    def in_map(row):
        return (row >= 0) & (row < height)

    def fill(at):
        for j in range(at, at + GROUP):
            add = lift_col * demand[j : j + 1, :]
            inp[j] = (gath[j].astype(F32) + add).astype(BF16)

    col = lane + ci * own_cols - margin
    col_ok = ((col >= 0) & (col < cols)).astype(F32)

    def gathered(ref, at, dilation):
        return jnp.concatenate(
            [
                jnp.concatenate([ref[at + j + u * dilation] for u in range(3)], axis=0)
                for j in range(GROUP)
            ],
            axis=1,
        )

    def conv(ref, at, weights, dilation):
        result = jnp.dot(weights[...], gathered(ref, at, dilation), preferred_element_type=F32)
        parts = []
        for j in range(GROUP):
            one = result[:, j * LANES : (j + 1) * LANES]
            parts.append(
                one[chan : 2 * chan]
                + pltpu.roll(one[:chan], dilation, 1)
                + pltpu.roll(one[2 * chan :], LANES - dilation, 1)
            )
        return parts

    def keep_of(row):
        return col_ok * in_map(row).astype(F32)

    def first(at):
        keep = keep_of(top - 20 + at)
        for j, value in enumerate(conv(inp, at, wm1, 4)):
            pre[at + j] = value
            hid[at + j] = (value * jax.nn.sigmoid(value) * keep).astype(BF16)

    def second(at):
        keep = keep_of(top - 12 + at)
        for j, value in enumerate(conv(hid, at, wm2, 8)):
            sec[at + j] = (jax.nn.sigmoid(value) * keep).astype(BF16)

    def third(at):
        keep = keep_of(top - 4 + at)
        for j, value in enumerate(conv(sec, at, wm3, 8)):
            p = pre[at + j + 16]
            s = jax.nn.sigmoid(p)
            gpre[at + j] = (value * s * (1.0 + p * (1.0 - s)) * keep).astype(BF16)

    here, done = set(), set()
    for stage in stages:
        fresh = set()
        for delta in stage:
            feat_wait(delta)
            low, count, at = spans(delta)
            fresh |= set(range(at, at + count))
        here |= fresh
        for at in range(0, in_rows, GROUP):
            if at in fresh:
                fill(at)
        for at in range(0, rows + 40, GROUP):
            if at not in done and all(at + j in here for j in range(GROUP + 8)):
                done.add(at)
                first(at)
    for at in range(0, rows + 24, GROUP):
        second(at)
    for at in range(0, rows + 8, GROUP):
        third(at)

    owned = ((lane >= margin) & (lane < margin + own_cols)).astype(F32)
    for g in range(rows // GROUP):
        at = g * GROUP
        result = jnp.dot(wm4[...], gathered(gpre, at, 4), preferred_element_type=F32)
        result = result[0:8] + result[8:16] + result[16:24]
        for j in range(GROUP):
            one = result[:, j * LANES : (j + 1) * LANES]
            line = (
                one[1:2]
                + pltpu.roll(one, 4, 1)[0:1]
                + pltpu.roll(one, LANES - 4, 1)[2:3]
            )
            gown[at + j : at + j + 1, :] = line * owned

    def grad_copy(step):
        to = wrap(ti + step, tiles)
        return pltpu.make_async_remote_copy(
            src_ref=gown, dst_ref=gall.at[pl.ds(pl.multiple_of(ti * rows, rows), rows)],
            send_sem=gsend_sem.at[step], recv_sem=grecv_sem.at[step],
            device_id=(to, ci), device_id_type=MESH,
        )

    def grad_arrival(step):
        come = wrap(ti + tiles - step, tiles)
        dst = gall.at[pl.ds(pl.multiple_of(come * rows, rows), rows)]
        return pltpu.make_async_remote_copy(
            src_ref=gown, dst_ref=dst,
            send_sem=gsend_sem.at[step], recv_sem=grecv_sem.at[step],
            device_id=(wrap(ti + step, tiles), ci), device_id_type=MESH,
        )

    each(1, tiles, lambda s: grad_copy(s).start())
    mine = pltpu.make_async_copy(
        gown, gall.at[pl.ds(pl.multiple_of(ti * rows, rows), rows)], gown_sem
    )
    mine.start()
    mine.wait()
    each(1, tiles, lambda s: grad_arrival(s).wait_recv())

    entry_sum = jnp.zeros((entries, LANES), F32)
    for i in range(TILE_ROWS):
        grads = gall[pl.ds(i, map_blocks, stride=TILE_ROWS), :]
        high, low_ = split(grads, 2)
        rows_of = jnp.dot(block_hot[...], high, preferred_element_type=F32)
        rows_of = rows_of + jnp.dot(block_hot[...], low_, preferred_element_type=F32)
        entry_sum = entry_sum + rows_of * fmask[:, i * LANES : (i + 1) * LANES].astype(F32)
    entry_grad = jnp.sum(entry_sum, axis=1, keepdims=True)
    pin_grad = jnp.sum(same_net[...] * entry_grad, axis=0, keepdims=True)
    pieces = jnp.concatenate([p.astype(F32) for p in split(by_dest[...] * pin_grad, 3)], axis=0).astype(BF16)
    cells = lax.dot_general(
        pieces, by_cell[...], (((1,), (1,)), ((), ())), preferred_element_type=F32
    )
    cells = cells[:dest_rows] + cells[dest_rows : 2 * dest_rows] + cells[2 * dest_rows :]
    for t in range(tiles):
        csend[t] = cells[t : t + 1, :]

    def cell_copy(step, to):
        return pltpu.make_async_remote_copy(
            src_ref=csend.at[to[0]], dst_ref=crecv.at[step],
            send_sem=csend_sem, recv_sem=crecv_sem,
            device_id=to, device_id_type=MESH,
        )

    each_peer(lambda n, who: cell_copy(n, who).start())

    for delta in sum(stages, []):
        for k in range(chans):
            if delta == 0:
                if k:
                    feat_copy(delta, k).wait_send()
            else:
                @pl.when((ti + delta >= 0) & (ti + delta < tiles))
                def _(delta=delta, k=k):
                    feat_copy(delta, k).wait_send()
    each(1, tiles, lambda s: grad_copy(s).wait_send())
    arrived = crecv.at[pl.ds(1, others)]
    pltpu.make_async_remote_copy(
        src_ref=arrived, dst_ref=arrived, send_sem=csend_sem, recv_sem=crecv_sem,
        device_id=(ti, wrap(ci + 1, chans)), device_id_type=MESH,
    ).wait()
    out[...] = csend[ti] + jnp.sum(crecv[1:], axis=0)


def solution(mesh):
    tiles, chans = mesh.shape["tile"], mesh.shape["chan"]

    def local(
        feat, lift, w4, w8, frac, target, owner, net_e, weight, net_p, cell,
    ):
        rows, chan_own, cols = feat.shape
        chan = chan_own * chans
        entries = frac.shape[0]
        pins = weight.shape[0]
        in_rows = rows + 2 * HALO
        reach = -(-HALO // rows)
        height = rows * tiles
        blocks = -(-(height + 2 * HALO) // (8 * TILE_ROWS)) * 8
        vm = pltpu.VMEM
        dma = pltpu.SemaphoreType.DMA
        result = pl.pallas_call(
            functools.partial(kernel, tiles, chans),
            out_shape=jax.ShapeDtypeStruct((1, LANES), F32),
            in_specs=[pl.BlockSpec(memory_space=pltpu.HBM)] * 11,
            out_specs=pl.BlockSpec(memory_space=pltpu.VMEM),
            scratch_shapes=[
                vm(feat.shape, BF16),
                vm((1, chan), F32),
                vm(w4.shape, BF16),
                vm(w8.shape, BF16),
                vm(frac.shape, BF16),
                vm((1, entries), jnp.int32),
                vm((1, entries), jnp.int32),
                vm((1, entries), jnp.int32),
                vm((1, pins), F32),
                vm((1, pins), jnp.int32),
                vm((1, pins), jnp.int32),
                dma((11,)),
                vm((chans, rows, chan_own, LANES), BF16),
                vm((in_rows, chan, LANES), BF16),
                vm((in_rows, chan, LANES), BF16),
                vm((rows + 40, chan, LANES), F32),
                vm((rows + 40, chan, LANES), BF16),
                vm((rows + 24, chan, LANES), BF16),
                vm((rows + 8, chan, LANES), BF16),
                vm((3 * chan, 3 * chan), BF16),
                vm((3 * chan, 3 * chan), BF16),
                vm((3 * chan, 3 * chan), BF16),
                vm((32, 3 * chan), BF16),
                vm((entries, TILE_ROWS * LANES), BF16),
                vm((entries, height // TILE_ROWS), BF16),
                vm((entries, pins), F32),
                vm((max(8, tiles), pins), F32),
                vm((LANES, pins), BF16),
                vm((blocks * TILE_ROWS, LANES), F32),
                vm((blocks * TILE_ROWS, LANES), BF16),
                vm((tiles, in_rows, LANES), BF16),
                vm((in_rows, LANES), F32),
                vm((rows, LANES), F32),
                vm((height, LANES), F32),
                vm((tiles, 1, LANES), F32),
                vm((tiles * chans, 1, LANES), F32),
                dma((2 * reach + 1, chans)),
                dma((2 * reach + 1, chans)),
                dma(()),
                dma((tiles,)),
                dma((tiles,)),
                dma((tiles,)),
                dma((tiles,)),
                dma(()),
                dma(()),
                dma(()),
            ],
            compiler_params=pltpu.CompilerParams(collective_id=0, has_side_effects=True),
        )(
            feat, lift.reshape(1, chan), w4, w8, frac, target.reshape(1, entries),
            owner.reshape(1, entries), net_e.reshape(1, entries), weight.reshape(1, pins),
            net_p.reshape(1, pins), cell.reshape(1, pins),
        )
        return result[0, :CELL_DEV]

    in_specs = (
        P("tile", "chan", None), P(), P(), P(),
        P("tile", None), P("tile", None),
        P("tile"), P("tile"), P("tile"), P("tile"), P("tile"),
    )
    return jax.shard_map(
        local, mesh=mesh, in_specs=in_specs, out_specs=P("tile"), check_vma=False
    )
```
